256 devices in a mesh: slab: 128 (over y, x, z), kv: 2 (over core).
Axes of the slice: x: 4, y: 4, z: 8, core: 2. Of those that a mesh axis runs over, the one named last changes fastest.
Arguments:
- queries: bfloat16 [131072, 512], P('slab'), may hold values from -6 to 6
- grad_out: bfloat16 [131072, 512], P('slab'), may hold values from -6 to 6
- attn_out: bfloat16 [131072, 512], P('slab'), may hold values from -6 to 6
- row_lse: float32 [131072], P('slab'), may hold values from 5.5 to 7.5
- keys: bfloat16 [2, 2048, 512], P('kv', 'slab'), may hold values from -6 to 6
- values: bfloat16 [2, 2048, 512], P('kv', 'slab'), may hold values from -6 to 6
Outputs:
- grad_queries: bfloat16 [131072, 512], P('slab', 'kv')
- grad_keys: bfloat16 [2, 2048, 512], P('kv', 'slab')
- grad_values: bfloat16 [2, 2048, 512], P('kv', 'slab')
The draws below stay inside these ranges and needn't reach their ends.
All inputs are finite; a program needn't handle non-finite values.
Results may differ from the reference program's by a relative error of at most 0.005.
Values may be sent and summed in bfloat16 or wider, within the bound.
No kernel may reach another device: no remote copies, remote signals or barrier semaphores. Data moves between devices by JAX's collectives and lax.ppermute only.
A program may use at most 128 MiB of HBM per device.

```python
import jax
import jax.numpy as jnp
from jax import lax

C = 512
TOK_DEV = 1024
KPANEL = 2048
TOKENS = 131072
N_SLAB = 128
N_KV = 2


def shard_levels(own_key, dims, shards, low, high):
    loudness = 1.0
    for axis_at, shards_of in shards:
        heights = jax.random.uniform(jax.random.fold_in(jax.random.fold_in(own_key, 6), axis_at), (shards_of,), jnp.float32, low / len(shards), high / len(shards))
        loudness = loudness * jnp.repeat(jnp.exp(heights), dims[axis_at] // shards_of).reshape((-1,) + (1,) * (len(dims) - 1 - axis_at))
    return loudness


def bell_draw(key, extent, scale, limit, shards=(), kind=jnp.bfloat16):
    result = jax.random.normal(key, extent, jnp.float32) * scale
    if len(shards) > 0:
        result = shard_levels(key, extent, shards, -0.22, 0.18) * result
    return jnp.clip(result, min=-limit, max=limit).astype(kind)


def setup_inputs(seed: int = 0) -> dict:
    key_of = jax.random.split(jax.random.key(seed), 7)
    queries = bell_draw(key_of[0], (TOKENS, C), 1.0, 6.0, ((0, 128),))
    grad_out = bell_draw(key_of[1], (TOKENS, C), 1.0, 6.0, ((0, 128),))
    attn_out = bell_draw(key_of[2], (TOKENS, C), 1.0, 6.0, ((0, 128),))
    row_lse = jnp.clip(5.5 + 2.0 * jax.random.uniform(key_of[3], (TOKENS,), jnp.float32) ** shard_levels(key_of[3], (TOKENS,), ((0, 128),), -0.2, 0.2), 5.5, 7.5)
    keys = bell_draw(key_of[4], (N_KV, KPANEL, C), 1.0, 6.0, ((0, 2), (1, 128)))
    values = bell_draw(key_of[5], (N_KV, KPANEL, C), 1.0, 6.0, ((0, 2), (1, 128)))
    return {"queries": queries, "grad_out": grad_out, "attn_out": attn_out, "row_lse": row_lse, "keys": keys, "values": values}


def reference(queries, grad_out, attn_out, row_lse, keys, values):
    score_scale = C ** -0.5

    def one_block(carry, block_index):
        grad_keys_acc, grad_values_acc = carry
        start = (block_index * TOK_DEV).astype(jnp.int32)
        query_rows = lax.dynamic_slice_in_dim(queries, start, TOK_DEV, 0)
        grad_rows = lax.dynamic_slice_in_dim(grad_out, start, TOK_DEV, 0)
        out_rows = lax.dynamic_slice_in_dim(attn_out, start, TOK_DEV, 0)
        lse_rows = lax.dynamic_slice_in_dim(row_lse, start, TOK_DEV, 0)
        stats = jnp.sum(grad_rows.astype(jnp.float32) * out_rows.astype(jnp.float32), axis=1)
        grad_query = jnp.zeros((TOK_DEV, C), jnp.float32)
        for panel in range(N_KV):
            panel_keys = keys[panel]
            panel_values = values[panel]
            scores = jnp.dot(query_rows, panel_keys.T, preferred_element_type=jnp.float32) * score_scale
            probs = jnp.exp(scores - lse_rows[:, None])
            probs_low = probs.astype(jnp.bfloat16)
            dprobs = jnp.dot(grad_rows, panel_values.T, preferred_element_type=jnp.float32)
            dscores = (probs * (dprobs - stats[:, None])).astype(jnp.bfloat16)
            grad_query = grad_query + jnp.dot(dscores, panel_keys, preferred_element_type=jnp.float32) * score_scale
            key_term = jnp.dot(dscores.T, query_rows, preferred_element_type=jnp.float32) * score_scale
            value_term = jnp.dot(probs_low.T, grad_rows, preferred_element_type=jnp.float32)
            grad_keys_acc = grad_keys_acc.at[panel].add(key_term)
            grad_values_acc = grad_values_acc.at[panel].add(value_term)
        return (grad_keys_acc, grad_values_acc), grad_query.astype(jnp.bfloat16)

    empty = jnp.zeros((N_KV, KPANEL, C), jnp.float32)
    (grad_keys_sum, grad_values_sum), grad_blocks = lax.scan(one_block, (empty, empty), jnp.arange(N_SLAB, dtype=jnp.int32))
    grad_queries = grad_blocks.reshape(TOKENS, C)
    return grad_queries, grad_keys_sum.astype(jnp.bfloat16), grad_values_sum.astype(jnp.bfloat16)
```

```python
import jax
import jax.numpy as jnp
from jax import lax
from jax.sharding import Mesh
from jax.sharding import PartitionSpec as P

SLAB = ("slab_0", "slab_1", "slab_2")
F32 = jnp.float32
BF16 = jnp.bfloat16


def neighbour(i, n, turn):
    if turn == 0:
        return i ^ 1
    return (i - 1) % n if i % 2 == 0 else (i + 1) % n


def trade(x, axis, turn):
    n = lax.axis_size(axis)
    pairs = []
    for i in range(n):
        for core in range(2):
            j = neighbour(i, n, (turn + core) % 2)
            pairs.append((2 * i + core, 2 * j + core))
    return lax.ppermute(x, (axis, "kv"), pairs)


def swap(x):
    return lax.ppermute(x, "kv", [(0, 1), (1, 0)])


def contract_last(left, right):
    return lax.dot_general(left, right, (((1,), (1,)), ((), ())), preferred_element_type=F32)


def contract_first(left, right):
    return lax.dot_general(left, right, (((0,), (0,)), ((), ())), preferred_element_type=F32)


def three_parts(v):
    hi = lax.reduce_precision(v, 8, 7)
    rest = v - hi
    mid = lax.reduce_precision(rest, 8, 7)
    low = rest - mid
    return jnp.stack([hi, mid, low]).astype(BF16)


def on_device(queries, grad_out, attn_out, row_lse, keys, values):
    tokens, channels = queries.shape
    scale = channels ** (-0.5)
    core = lax.axis_index("kv")
    half = tokens // 2

    k0 = jnp.concatenate([keys[0], values[0]], axis=1)
    z1 = trade(k0, "slab_2", 0)
    z2 = trade(jnp.concatenate([k0, z1]), "slab_2", 1)
    z3 = trade(z2, "slab_2", 0)
    z4 = trade(z3, "slab_2", 1)
    zall = jnp.concatenate([k0, z1, z2, z3, z4])
    y1 = trade(zall, "slab_0", 0)
    y2 = trade(jnp.concatenate([zall, y1]), "slab_0", 1)
    mine = jnp.concatenate([zall, y1, y2])
    theirs = swap(mine)

    def my_half(a):
        return lax.dynamic_slice_in_dim(a, core * half, half, 0)

    q, g, o, lse = my_half(queries), my_half(grad_out), my_half(attn_out), my_half(row_lse)
    stats = jnp.sum(g.astype(F32) * o.astype(F32), axis=1)
    extra = three_parts(jnp.concatenate([lse, stats]))
    extra = jnp.pad(extra, ((0, 13), (0, 0)))
    pack0 = jnp.concatenate([jnp.concatenate([q, g], axis=1), extra])
    pack1 = trade(pack0, "slab_1", 0)
    pack2 = trade(pack0, "slab_1", 1)
    pack3 = trade(pack1, "slab_1", 1)

    def work(pack, panel):
        qs, gs = pack[:half, :channels], pack[:half, channels:]
        both = jnp.sum(pack[half : half + 3].astype(F32), axis=0)
        lse_t, stats_t = both[:half], both[half:]
        k, v = panel[:, :channels], panel[:, channels:]
        probs = jnp.exp(contract_last(qs, k) * scale - lse_t[:, None])
        dscores = (probs * (contract_last(gs, v) - stats_t[:, None])).astype(BF16)
        dq = jnp.dot(dscores, k, preferred_element_type=F32)
        dk = contract_first(dscores, qs)
        dv = contract_first(probs.astype(BF16), gs)
        return dq, jnp.concatenate([dk, dv], axis=1)

    dqs, mine_sum, theirs_sum = [], 0.0, 0.0
    for pack in (pack0, pack1, pack2, pack3):
        dq_a, m = work(pack, mine)
        dq_b, t = work(pack, theirs)
        dqs.append(dq_a + dq_b)
        mine_sum, theirs_sum = mine_sum + m, theirs_sum + t

    got2 = trade(dqs[2].astype(BF16), "slab_1", 1).astype(F32)
    got3 = trade(dqs[3].astype(BF16), "slab_1", 1).astype(F32)
    got1 = trade((dqs[1] + got3).astype(BF16), "slab_1", 0).astype(F32)
    dq = ((dqs[0] + got2 + got1) * scale).astype(BF16)
    width = channels // 2
    keep = lax.dynamic_slice_in_dim(dq, core * width, width, 1)
    away = swap(lax.dynamic_slice_in_dim(dq, (1 - core) * width, width, 1))
    grad_queries = jnp.where(core == 0, jnp.concatenate([keep, away]), jnp.concatenate([away, keep]))

    total = mine_sum + swap(theirs_sum.astype(BF16)).astype(F32)
    n1, n = keys.shape[1], keys.shape[1] * 8
    total = total[: 2 * n] + trade(total[2 * n :].astype(BF16), "slab_0", 1).astype(F32)
    total = total[:n] + trade(total[n:].astype(BF16), "slab_0", 0).astype(F32)
    t0, t2, t3, t4 = total[: 2 * n1], total[2 * n1 : 4 * n1], total[4 * n1 : 6 * n1], total[6 * n1 :]
    t3 = t3 + trade(t4.astype(BF16), "slab_2", 1).astype(F32)
    t2 = t2 + trade(t3.astype(BF16), "slab_2", 0).astype(F32)
    t0 = t0 + trade(t2.astype(BF16), "slab_2", 1).astype(F32)
    own = t0[:n1] + trade(t0[n1:].astype(BF16), "slab_2", 0).astype(F32)
    grad_keys = (own[:, :channels] * scale).astype(BF16)[None]
    grad_values = own[:, channels:].astype(BF16)[None]
    return (grad_queries, grad_keys, grad_values)


def solution(mesh):
    torus = Mesh(
        mesh.devices.reshape(4, 4, 8, mesh.shape["kv"]), ("slab_0", "slab_1", "slab_2", "kv")
    )
    placed = (
        P(SLAB, None),
        P(SLAB, None),
        P(SLAB, None),
        P(SLAB),
        P("kv", SLAB, None),
        P("kv", SLAB, None),
    )
    return jax.shard_map(
        on_device,
        mesh=torus,
        in_specs=placed,
        out_specs=(P(SLAB, "kv"), P("kv", SLAB, None), P("kv", SLAB, None)),
        check_vma=False,
    )
```

```python
import jax
import jax.numpy as jnp
from jax import lax
from jax.experimental import pallas as pl
from jax.experimental.pallas import tpu as pltpu
from jax.sharding import Mesh
from jax.sharding import PartitionSpec as P

SLAB = ("slab_0", "slab_1", "slab_2")
F32 = jnp.float32
BF16 = jnp.bfloat16


def neighbour(i, n, turn):
    if turn == 0:
        return i ^ 1
    return (i - 1) % n if i % 2 == 0 else (i + 1) % n


def trade(x, axis, turn):
    n = lax.axis_size(axis)
    pairs = []
    for i in range(n):
        for core in range(2):
            j = neighbour(i, n, (turn + core) % 2)
            pairs.append((2 * i + core, 2 * j + core))
    return lax.ppermute(x, (axis, "kv"), pairs)


def swap(x):
    return lax.ppermute(x, "kv", [(0, 1), (1, 0)])


def three_parts(v):
    hi = lax.reduce_precision(v, 8, 7)
    rest = v - hi
    mid = lax.reduce_precision(rest, 8, 7)
    low = rest - mid
    return jnp.stack([hi, mid, low]).astype(BF16)


def dot(left, right, ld, rd):
    return lax.dot_general(left, right, (((ld,), (rd,)), ((), ())), preferred_element_type=F32)


def block_kernel(n_packs, first, add, pack_refs, panel_ref, dq_in, sum_in, dq_out, sum_out):
    half, channels = dq_out[0].shape
    log2e = 1.4426950408889634
    scale = channels ** (-0.5) * log2e
    k, v = panel_ref[:, :channels], panel_ref[:, channels:]
    dk, dv = None, None
    for i in range(n_packs):
        q, g = pack_refs[i][:half, :channels], pack_refs[i][:half, channels:]
        both = jnp.sum(pack_refs[i][half:, :].astype(F32), axis=0, keepdims=True)
        lse, stats = both[:, :half] * log2e, both[:, half:]
        probs = jnp.exp2(dot(k, q, 1, 1) * scale - lse)
        dscores = (probs * (dot(v, g, 1, 1) - stats)).astype(BF16)
        dk_i = dot(dscores, q, 1, 0)
        dv_i = dot(probs.astype(BF16), g, 1, 0)
        dk = dk_i if dk is None else dk + dk_i
        dv = dv_i if dv is None else dv + dv_i
        dq = dot(dscores, k, 0, 0)
        dq_out[i][...] = dq if first else dq_in[i][...] + dq
    if add:
        dk, dv = dk + sum_in[:, :channels], dv + sum_in[:, channels:]
    sum_out[:, :channels] = dk.astype(sum_out.dtype)
    sum_out[:, channels:] = dv.astype(sum_out.dtype)


def block_work(packs, panel, dqs, total, out_type):
    n_packs, first, add = len(packs), dqs is None, total is not None
    half, channels = packs[0].shape[0] - 16, packs[0].shape[1] // 2
    keys = panel.shape[0]

    def body(*refs):
        refs = list(refs)
        pack_refs = [refs.pop(0) for _ in range(n_packs)]
        panel_ref = refs.pop(0)
        dq_in = None if first else [refs.pop(0) for _ in range(n_packs)]
        sum_in = refs.pop(0) if add else None
        dq_out = [refs.pop(0) for _ in range(n_packs)]
        block_kernel(n_packs, first, add, pack_refs, panel_ref, dq_in, sum_in, dq_out, refs.pop(0))

    args = [*packs, panel, *([] if first else dqs), *([total] if add else [])]
    aliases = {} if first else {n_packs + 1 + i: i for i in range(n_packs)}
    if add and out_type == F32:
        aliases[len(args) - 1] = n_packs
    vmem = pl.BlockSpec(memory_space=pltpu.VMEM)
    out = pl.pallas_call(
        body,
        out_shape=[jax.ShapeDtypeStruct((half, channels), F32)] * n_packs
        + [jax.ShapeDtypeStruct((keys, 2 * channels), out_type)],
        in_specs=[vmem] * len(args),
        out_specs=[vmem] * (n_packs + 1),
        input_output_aliases=aliases,
        cost_estimate=pl.CostEstimate(
            flops=10 * n_packs * half * keys * channels,
            bytes_accessed=2 * n_packs * half * channels * 2,
            transcendentals=n_packs * half * keys,
        ),
        compiler_params=pltpu.CompilerParams(vmem_limit_bytes=16 * 1024 * 1024),
    )(*args)
    return list(out[:n_packs]), out[n_packs]


def steps(queries, grad_out, attn_out, row_lse, keys, values):
    tokens, channels = queries.shape
    scale = channels ** (-0.5)
    core = lax.axis_index("kv")
    half = tokens // 2

    def my_half(a):
        return lax.dynamic_slice_in_dim(a, core * half, half, 0)

    q, g, o, lse = my_half(queries), my_half(grad_out), my_half(attn_out), my_half(row_lse)
    stats = jnp.sum(g.astype(F32) * o.astype(F32), axis=1)
    extra = three_parts(jnp.concatenate([lse, stats]))
    extra = jnp.pad(extra, ((0, 13), (0, 0)))
    pack0 = jnp.concatenate([jnp.concatenate([q, g], axis=1), extra])
    pack1 = trade(pack0, "slab_1", 0)
    pack2 = trade(pack0, "slab_1", 1)
    pack3 = trade(pack1, "slab_1", 1)

    k0 = jnp.concatenate([keys[0], values[0]], axis=1)
    z1 = trade(k0, "slab_2", 0)
    z2 = trade(jnp.concatenate([k0, z1]), "slab_2", 1)
    z3 = trade(z2, "slab_2", 0)
    z4 = trade(z3, "slab_2", 1)
    zall = jnp.concatenate([k0, z1, z2, z3, z4])
    y1 = trade(zall, "slab_0", 0)
    near = jnp.concatenate([zall, y1])
    far = trade(near, "slab_0", 1)
    near_other = swap(near)
    far_other = swap(far)

    a = [pack0, pack1]
    b = [pack2, pack3]
    dqa, near_sum = block_work(a, near, None, None, F32)
    dqa, near_osum = block_work(a, near_other, dqa, None, F32)
    dqa, far_sum = block_work(a, far, dqa, None, F32)
    dqa, far_osum = block_work(a, far_other, dqa, None, F32)
    dqb, far_osum = block_work(b, far_other, None, far_osum, BF16)
    dqb, far_sum = block_work(b, far, dqb, far_sum, F32)
    dqb, near_osum = block_work(b, near_other, dqb, near_osum, BF16)
    dqb, near_sum = block_work(b, near, dqb, near_sum, F32)

    far_sum = far_sum + swap(far_osum).astype(F32)
    near_sum = near_sum + swap(near_osum).astype(F32)
    n1, n = keys.shape[1], keys.shape[1] * 8
    total = near_sum + trade(far_sum.astype(BF16), "slab_0", 1).astype(F32)
    total = total[:n] + trade(total[n:].astype(BF16), "slab_0", 0).astype(F32)
    t0, t2, t3, t4 = total[: 2 * n1], total[2 * n1 : 4 * n1], total[4 * n1 : 6 * n1], total[6 * n1 :]
    t3 = t3 + trade(t4.astype(BF16), "slab_2", 1).astype(F32)
    t2 = t2 + trade(t3.astype(BF16), "slab_2", 0).astype(F32)
    t0 = t0 + trade(t2.astype(BF16), "slab_2", 1).astype(F32)
    own = t0[:n1] + trade(t0[n1:].astype(BF16), "slab_2", 0).astype(F32)
    grad_keys = (own[:, :channels] * scale).astype(BF16)[None]
    grad_values = own[:, channels:].astype(BF16)[None]

    got3 = trade(dqb[1].astype(BF16), "slab_1", 1).astype(F32)
    got2 = trade(dqb[0].astype(BF16), "slab_1", 1).astype(F32)
    got1 = trade((dqa[1] + got3).astype(BF16), "slab_1", 0).astype(F32)
    dq = ((dqa[0] + got2 + got1) * scale).astype(BF16)
    width = channels // 2
    keep = lax.dynamic_slice_in_dim(dq, core * width, width, 1)
    away = swap(lax.dynamic_slice_in_dim(dq, (1 - core) * width, width, 1))
    grad_queries = jnp.where(core == 0, jnp.concatenate([keep, away]), jnp.concatenate([away, keep]))
    return (grad_queries, grad_keys, grad_values)


def solution(mesh):
    torus = Mesh(
        mesh.devices.reshape(4, 4, 8, mesh.shape["kv"]), ("slab_0", "slab_1", "slab_2", "kv")
    )
    placed = (
        P(SLAB, None),
        P(SLAB, None),
        P(SLAB, None),
        P(SLAB),
        P("kv", SLAB, None),
        P("kv", SLAB, None),
    )
    return jax.shard_map(
        steps,
        mesh=torus,
        in_specs=placed,
        out_specs=(P(SLAB, "kv"), P("kv", SLAB, None), P("kv", SLAB, None)),
        check_vma=False,
    )
```

```python
import functools

import jax
import jax.numpy as jnp
from jax import lax
from jax.experimental import pallas as pl
from jax.experimental.pallas import tpu as pltpu
from jax.sharding import Mesh
from jax.sharding import PartitionSpec as P

SLAB = ("slab_0", "slab_1", "slab_2")
F32 = jnp.float32
BF16 = jnp.bfloat16


def neighbour(i, n, turn):
    if turn == 0:
        return i ^ 1
    return (i - 1) % n if i % 2 == 0 else (i + 1) % n


def trade(x, axis, turn):
    n = lax.axis_size(axis)
    pairs = []
    for i in range(n):
        for core in range(2):
            j = neighbour(i, n, (turn + core) % 2)
            pairs.append((2 * i + core, 2 * j + core))
    return lax.ppermute(x, (axis, "kv"), pairs)


def swap(x):
    return lax.ppermute(x, "kv", [(0, 1), (1, 0)])


def across(x):
    return lax.all_to_all(x, "slab_2", 0, 0, tiled=True)


def pack_kernel(
    core_ref, q_hbm, g_hbm, o_hbm, lse_hbm, k_hbm, v_hbm, out_ref, own_ref, o_half, lse_ref, kv_ref, sems
):
    half, channels = o_half.shape
    core = core_ref[0]
    piece = 128
    n = half // piece
    copies = []
    for i in range(n):
        rows = pl.ds(pl.multiple_of(core * half + i * piece, piece), piece)
        to = slice(i * piece, (i + 1) * piece)
        copies.append(
            (
                pltpu.make_async_copy(g_hbm.at[rows, :], out_ref.at[to, channels:], sems.at[i]),
                pltpu.make_async_copy(o_hbm.at[rows, :], o_half.at[to, :], sems.at[n + i]),
                pltpu.make_async_copy(q_hbm.at[rows, :], out_ref.at[to, :channels], sems.at[2 * n + i]),
            )
        )
    small = [
        pltpu.make_async_copy(lse_hbm, lse_ref, sems.at[3 * n]),
        pltpu.make_async_copy(k_hbm.at[0], kv_ref.at[:, :channels], sems.at[3 * n + 1]),
        pltpu.make_async_copy(v_hbm.at[0], kv_ref.at[:, channels:], sems.at[3 * n + 2]),
    ]
    for copy in small:
        copy.start()
    for trio in copies:
        trio[0].start()
        trio[1].start()
    for trio in copies:
        trio[2].start()
    for copy in small:
        copy.wait()
    for i in range(own_ref.shape[0]):
        own_ref[i] = kv_ref[...]

    def line(first):
        return jnp.concatenate([lse_ref[i : i + 1, :] for i in range(first, first + n)], axis=1)

    lse = jnp.where(core == 0, line(0), line(n))
    pieces = []
    for i in range(n):
        copies[i][0].wait()
        copies[i][1].wait()
        to = slice(i * piece, (i + 1) * piece)
        product = out_ref[to, channels:].astype(F32) * o_half[to, :].astype(F32)
        column = jnp.sum(product, axis=1, keepdims=True)
        pieces.append(jnp.transpose(jnp.broadcast_to(column, (piece, 128)))[:1, :])
    stats = jnp.concatenate(pieces, axis=1)
    row = lax.broadcasted_iota(jnp.int32, (16, half), 0)
    for at, v in ((0, lse), (half, stats)):
        hi = v.astype(BF16).astype(F32)
        mid = (v - hi).astype(BF16).astype(F32)
        low = v - hi - mid
        terms = jnp.where(row == 0, hi, jnp.where(row == 1, mid, jnp.where(row == 2, low, 0.0)))
        out_ref[half:, at : at + half] = terms.astype(BF16)
    for trio in copies:
        trio[2].wait()


def make_pack(core, queries, grad_out, attn_out, row_lse, keys, values):
    tokens, channels = queries.shape
    half = tokens // 2
    arrays = (queries, grad_out, attn_out, row_lse.reshape(-1, 128), keys, values)
    arrays = [pltpu.with_memory_space_constraint(a, pltpu.HBM) for a in arrays]
    hbm = pl.BlockSpec(memory_space=pltpu.HBM)
    vmem = pl.BlockSpec(memory_space=pltpu.VMEM)
    rows = keys.shape[1]
    return pl.pallas_call(
        pack_kernel,
        out_shape=[
            jax.ShapeDtypeStruct((half + 16, 2 * channels), BF16),
            jax.ShapeDtypeStruct((8, rows, 2 * channels), BF16),
        ],
        in_specs=[pl.BlockSpec(memory_space=pltpu.SMEM)] + [hbm] * 6,
        out_specs=[vmem, vmem],
        scratch_shapes=[
            pltpu.VMEM((half, channels), BF16),
            pltpu.VMEM((tokens // 128, 128), F32),
            pltpu.VMEM((rows, 2 * channels), BF16),
            pltpu.SemaphoreType.DMA((15,)),
        ],
        compiler_params=pltpu.CompilerParams(vmem_limit_bytes=16 * 1024 * 1024),
        name="pack",
    )(core.reshape(1), *arrays)


def finish_kernel(scale, parts_ref, k_ref, v_ref):
    channels = k_ref.shape[2]
    own = jnp.sum(parts_ref[...].astype(F32), axis=0)
    k_ref[0] = (own[:, :channels] * scale).astype(BF16)
    v_ref[0] = own[:, channels:].astype(BF16)


def finish(parts, scale):
    rows, channels = parts.shape[1], parts.shape[2] // 2
    return pl.pallas_call(
        functools.partial(finish_kernel, scale),
        out_shape=[jax.ShapeDtypeStruct((1, rows, channels), BF16)] * 2,
        compiler_params=pltpu.CompilerParams(vmem_limit_bytes=4 * 1024 * 1024),
        name="finish",
    )(parts)


def dot(left, right, ld, rd):
    return lax.dot_general(left, right, (((ld,), (rd,)), ((), ())), preferred_element_type=F32)


def block_kernel(n_packs, first, add, pack_refs, panel_ref, dq_in, sum_in, dq_out, sum_out):
    half, channels = dq_out[0].shape
    log2e = 1.4426950408889634
    scale = channels ** (-0.5) * log2e
    k, v = panel_ref[:, :channels], panel_ref[:, channels:]
    dk, dv = None, None
    for i in range(n_packs):
        q, g = pack_refs[i][:half, :channels], pack_refs[i][:half, channels:]
        both = jnp.sum(pack_refs[i][half:, :].astype(F32), axis=0, keepdims=True)
        lse, stats = both[:, :half] * log2e, both[:, half:]
        probs = jnp.exp2(dot(k, q, 1, 1) * scale - lse)
        dscores = (probs * (dot(v, g, 1, 1) - stats)).astype(BF16)
        dk_i = dot(dscores, q, 1, 0)
        dv_i = dot(probs.astype(BF16), g, 1, 0)
        dk = dk_i if dk is None else dk + dk_i
        dv = dv_i if dv is None else dv + dv_i
        dq = dot(dscores, k, 0, 0)
        dq_out[i][...] = dq if first else dq_in[i][...] + dq
    if add:
        dk, dv = dk + sum_in[:, :channels], dv + sum_in[:, channels:]
    sum_out[:, :channels] = dk.astype(sum_out.dtype)
    sum_out[:, channels:] = dv.astype(sum_out.dtype)


def block_work(packs, panel, dqs, total, out_type):
    n_packs, first, add = len(packs), dqs is None, total is not None
    half, channels = packs[0].shape[0] - 16, packs[0].shape[1] // 2
    keys = panel.shape[0]

    def body(*refs):
        refs = list(refs)
        pack_refs = [refs.pop(0) for _ in range(n_packs)]
        panel_ref = refs.pop(0)
        dq_in = None if first else [refs.pop(0) for _ in range(n_packs)]
        sum_in = refs.pop(0) if add else None
        dq_out = [refs.pop(0) for _ in range(n_packs)]
        block_kernel(n_packs, first, add, pack_refs, panel_ref, dq_in, sum_in, dq_out, refs.pop(0))

    args = [*packs, panel, *([] if first else dqs), *([total] if add else [])]
    aliases = {} if first else {n_packs + 1 + i: i for i in range(n_packs)}
    if add and out_type == F32:
        aliases[len(args) - 1] = n_packs
    vmem = pl.BlockSpec(memory_space=pltpu.VMEM)
    out = pl.pallas_call(
        body,
        out_shape=[jax.ShapeDtypeStruct((half, channels), F32)] * n_packs
        + [jax.ShapeDtypeStruct((keys, 2 * channels), out_type)],
        in_specs=[vmem] * len(args),
        out_specs=[vmem] * (n_packs + 1),
        input_output_aliases=aliases,
        cost_estimate=pl.CostEstimate(
            flops=10 * n_packs * half * keys * channels,
            bytes_accessed=2 * n_packs * half * channels * 2,
            transcendentals=n_packs * half * keys,
        ),
        compiler_params=pltpu.CompilerParams(vmem_limit_bytes=16 * 1024 * 1024),
    )(*args)
    return list(out[:n_packs]), out[n_packs]


def steps(queries, grad_out, attn_out, row_lse, keys, values):
    _, channels = queries.shape
    scale = channels ** (-0.5)
    core = lax.axis_index("kv")

    pack0, k0 = make_pack(core, queries, grad_out, attn_out, row_lse, keys, values)
    pack1 = trade(pack0, "slab_1", 0)
    pack2 = trade(pack0, "slab_1", 1)
    pack3 = trade(pack1, "slab_1", 1)

    zall = across(k0).reshape(-1, k0.shape[2])
    y1 = trade(zall, "slab_0", 0)
    near = jnp.concatenate([zall, y1])
    far = trade(near, "slab_0", 1)
    near_other = swap(near)
    far_other = swap(far)

    a = [pack0, pack1, pack2]
    b = [pack3]
    dqa, near_sum = block_work(a, near, None, None, F32)
    dqa, near_osum = block_work(a, near_other, dqa, None, F32)
    dqa, far_sum = block_work(a, far, dqa, None, F32)
    dqa, far_osum = block_work(a, far_other, dqa, None, F32)
    dqb, far_osum = block_work(b, far_other, None, far_osum, BF16)
    dqb, far_sum = block_work(b, far, dqb, far_sum, F32)
    dqb, near_osum = block_work(b, near_other, dqb, near_osum, BF16)
    dqb, near_sum = block_work(b, near, dqb, near_sum, F32)

    far_sum = far_sum + swap(far_osum).astype(F32)
    near_sum = near_sum + swap(near_osum).astype(F32)
    n1, n = keys.shape[1], keys.shape[1] * 8
    total = near_sum + trade(far_sum.astype(BF16), "slab_0", 1).astype(F32)
    total = total[:n] + trade(total[n:].astype(BF16), "slab_0", 0).astype(F32)
    parts = across(total.astype(BF16).reshape(8, n1, -1))
    grad_keys, grad_values = finish(parts, scale)

    got3 = trade(dqb[0].astype(BF16), "slab_1", 1).astype(F32)
    got2 = trade(dqa[2].astype(BF16), "slab_1", 1).astype(F32)
    got1 = trade((dqa[1] + got3).astype(BF16), "slab_1", 0).astype(F32)
    dq = ((dqa[0] + got2 + got1) * scale).astype(BF16)
    width = channels // 2
    keep = lax.dynamic_slice_in_dim(dq, core * width, width, 1)
    away = swap(lax.dynamic_slice_in_dim(dq, (1 - core) * width, width, 1))
    grad_queries = jnp.where(
        core == 0, jnp.concatenate([keep, away]), jnp.concatenate([away, keep])
    )
    return (grad_queries, grad_keys, grad_values)


def solution(mesh):
    torus = Mesh(
        mesh.devices.reshape(4, 4, 8, mesh.shape["kv"]), ("slab_0", "slab_1", "slab_2", "kv")
    )
    placed = (
        P(SLAB, None),
        P(SLAB, None),
        P(SLAB, None),
        P(SLAB),
        P("kv", SLAB, None),
        P("kv", SLAB, None),
    )
    return jax.shard_map(
        steps,
        mesh=torus,
        in_specs=placed,
        out_specs=(P(SLAB, "kv"), P("kv", SLAB, None), P("kv", SLAB, None)),
        check_vma=False,
    )
```

```python
import functools

import jax
import jax.numpy as jnp
from jax import lax
from jax.experimental import pallas as pl
from jax.experimental.pallas import tpu as pltpu
from jax.sharding import Mesh
from jax.sharding import PartitionSpec as P

SLAB = ("slab_0", "slab_1", "slab_2")
F32 = jnp.float32
BF16 = jnp.bfloat16


def neighbour(i, n, turn):
    if turn == 0:
        return i ^ 1
    return (i - 1) % n if i % 2 == 0 else (i + 1) % n


def trade(x, axis, turn):
    n = lax.axis_size(axis)
    pairs = []
    for i in range(n):
        for core in range(2):
            j = neighbour(i, n, (turn + core) % 2)
            pairs.append((2 * i + core, 2 * j + core))
    return lax.ppermute(x, (axis, "kv"), pairs)


def swap(x):
    return lax.ppermute(x, "kv", [(0, 1), (1, 0)])


def across(x):
    return lax.all_to_all(x, "slab_2", 0, 0, tiled=True)


def pack_kernel(
    core_ref, q_hbm, g_hbm, o_hbm, lse_hbm, k_hbm, v_hbm,
    out_ref, top_ref, low_ref, own_ref, o_half, lse_ref, kv_ref, sems,
):
    half, channels = o_half.shape
    core = core_ref[0]
    piece = 128
    n = half // piece
    copies = []
    for i in range(n):
        rows = pl.ds(pl.multiple_of(core * half + i * piece, piece), piece)
        to = slice(i * piece, (i + 1) * piece)
        copies.append(
            (
                pltpu.make_async_copy(g_hbm.at[rows, :], out_ref.at[to, channels:], sems.at[i]),
                pltpu.make_async_copy(o_hbm.at[rows, :], o_half.at[to, :], sems.at[n + i]),
                pltpu.make_async_copy(q_hbm.at[rows, :], out_ref.at[to, :channels], sems.at[2 * n + i]),
            )
        )
    small = [
        pltpu.make_async_copy(lse_hbm, lse_ref, sems.at[3 * n]),
        pltpu.make_async_copy(k_hbm.at[0], kv_ref.at[:, :channels], sems.at[3 * n + 1]),
        pltpu.make_async_copy(v_hbm.at[0], kv_ref.at[:, channels:], sems.at[3 * n + 2]),
    ]
    for copy in small:
        copy.start()
    for trio in copies:
        trio[0].start()
        trio[1].start()
    for trio in copies:
        trio[2].start()
    for copy in small:
        copy.wait()
    for i in range(own_ref.shape[0]):
        own_ref[i] = kv_ref[...]

    def line(first):
        return jnp.concatenate([lse_ref[i : i + 1, :] for i in range(first, first + n)], axis=1)

    lse = jnp.where(core == 0, line(0), line(n))
    pieces = []
    for i in range(n):
        copies[i][0].wait()
        copies[i][1].wait()
        to = slice(i * piece, (i + 1) * piece)
        product = out_ref[to, channels:].astype(F32) * o_half[to, :].astype(F32)
        column = jnp.sum(product, axis=1, keepdims=True)
        pieces.append(jnp.transpose(jnp.broadcast_to(column, (piece, 128)))[:1, :])
    stats = jnp.concatenate(pieces, axis=1)
    row = lax.broadcasted_iota(jnp.int32, (16, half), 0)
    for at, v in ((0, lse), (half, stats)):
        hi = v.astype(BF16).astype(F32)
        mid = (v - hi).astype(BF16).astype(F32)
        low = v - hi - mid
        terms = jnp.where(row == 0, hi, jnp.where(row == 1, mid, jnp.where(row == 2, low, 0.0)))
        out_ref[half:, at : at + half] = terms.astype(BF16)
    for trio in copies:
        trio[2].wait()
    cut = top_ref.shape[0]
    top_ref[...] = out_ref[:cut, :]
    low_ref[...] = out_ref[cut:, :]


def make_pack(core, queries, grad_out, attn_out, row_lse, keys, values):
    tokens, channels = queries.shape
    half = tokens // 2
    arrays = (queries, grad_out, attn_out, row_lse.reshape(-1, 128), keys, values)
    arrays = [pltpu.with_memory_space_constraint(a, pltpu.HBM) for a in arrays]
    hbm = pl.BlockSpec(memory_space=pltpu.HBM)
    vmem = pl.BlockSpec(memory_space=pltpu.VMEM)
    rows = keys.shape[1]
    return pl.pallas_call(
        pack_kernel,
        out_shape=[
            jax.ShapeDtypeStruct((half + 16, 2 * channels), BF16),
            jax.ShapeDtypeStruct((half // 2, 2 * channels), BF16),
            jax.ShapeDtypeStruct((half // 2 + 16, 2 * channels), BF16),
            jax.ShapeDtypeStruct((8, rows, 2 * channels), BF16),
        ],
        in_specs=[pl.BlockSpec(memory_space=pltpu.SMEM)] + [hbm] * 6,
        out_specs=[vmem] * 4,
        scratch_shapes=[
            pltpu.VMEM((half, channels), BF16),
            pltpu.VMEM((tokens // 128, 128), F32),
            pltpu.VMEM((rows, 2 * channels), BF16),
            pltpu.SemaphoreType.DMA((15,)),
        ],
        compiler_params=pltpu.CompilerParams(vmem_limit_bytes=16 * 1024 * 1024),
        name="pack",
    )(core.reshape(1), *arrays)


def split_sum_kernel(mine_ref, got_ref, kept_ref, sent_ref):
    n = kept_ref.shape[0]
    kept_ref[...] = mine_ref[:n, :] + got_ref[:n, :].astype(F32)
    sent_ref[...] = (mine_ref[n:, :] + got_ref[n:, :].astype(F32)).astype(BF16)


def split_sum(mine, got):
    vmem = pl.BlockSpec(memory_space=pltpu.VMEM)
    half = (mine.shape[0] // 2, mine.shape[1])
    return pl.pallas_call(
        split_sum_kernel,
        out_shape=[jax.ShapeDtypeStruct(half, F32), jax.ShapeDtypeStruct(half, BF16)],
        in_specs=[vmem, vmem],
        out_specs=[vmem, vmem],
        compiler_params=pltpu.CompilerParams(vmem_limit_bytes=4 * 1024 * 1024),
        name="split_sum",
    )(mine, got)


def rounded_sum_kernel(mine_ref, got_ref, out_ref):
    total = mine_ref[...] + got_ref[...].astype(F32)
    out_ref[...] = total.astype(BF16).reshape(out_ref.shape)


def rounded_sum(mine, got, rows):
    vmem = pl.BlockSpec(memory_space=pltpu.VMEM)
    return pl.pallas_call(
        rounded_sum_kernel,
        out_shape=jax.ShapeDtypeStruct((got.shape[0] // rows, rows, got.shape[1]), BF16),
        in_specs=[vmem, vmem],
        compiler_params=pltpu.CompilerParams(vmem_limit_bytes=4 * 1024 * 1024),
        name="rounded_sum",
    )(mine, got)


def finish_kernel(scale, parts_ref, k_ref, v_ref):
    channels = k_ref.shape[2]
    own = jnp.sum(parts_ref[...].astype(F32), axis=0)
    k_ref[0] = (own[:, :channels] * scale).astype(BF16)
    v_ref[0] = own[:, channels:].astype(BF16)


def finish(parts, scale):
    rows, channels = parts.shape[1], parts.shape[2] // 2
    return pl.pallas_call(
        functools.partial(finish_kernel, scale),
        out_shape=[jax.ShapeDtypeStruct((1, rows, channels), BF16)] * 2,
        compiler_params=pltpu.CompilerParams(vmem_limit_bytes=4 * 1024 * 1024),
        name="finish",
    )(parts)


def dot(left, right, ld, rd):
    return lax.dot_general(left, right, (((ld,), (rd,)), ((), ())), preferred_element_type=F32)


def block_kernel(n_packs, first, add, pack_refs, panel_ref, dq_in, sum_in, dq_out, sum_out):
    half, channels = dq_out[0].shape
    log2e = 1.4426950408889634
    scale = channels ** (-0.5) * log2e
    k, v = panel_ref[:, :channels], panel_ref[:, channels:]
    dk, dv = None, None
    for i in range(n_packs):
        parts = pack_refs[i]
        last = parts[-1].shape[0] - 16
        q = [p[:, :channels] for p in parts[:-1]] + [parts[-1][:last, :channels]]
        g = [p[:, channels:] for p in parts[:-1]] + [parts[-1][:last, channels:]]
        q = q[0] if len(q) == 1 else jnp.concatenate(q)
        g = g[0] if len(g) == 1 else jnp.concatenate(g)
        both = jnp.sum(parts[-1][last:, :].astype(F32), axis=0, keepdims=True)
        lse, stats = both[:, :half] * log2e, both[:, half:]
        probs = jnp.exp2(dot(k, q, 1, 1) * scale - lse)
        dscores = (probs * (dot(v, g, 1, 1) - stats)).astype(BF16)
        dk_i = dot(dscores, q, 1, 0)
        dv_i = dot(probs.astype(BF16), g, 1, 0)
        dk = dk_i if dk is None else dk + dk_i
        dv = dv_i if dv is None else dv + dv_i
        dq = dot(dscores, k, 0, 0)
        dq_out[i][...] = dq if first else dq_in[i][...] + dq
    if add:
        dk, dv = dk + sum_in[:, :channels], dv + sum_in[:, channels:]
    sum_out[:, :channels] = dk.astype(sum_out.dtype)
    sum_out[:, channels:] = dv.astype(sum_out.dtype)


def block_work(packs, panel, dqs, total, out_type):
    n_packs, first, add = len(packs), dqs is None, total is not None
    half, channels = sum(p.shape[0] for p in packs[0]) - 16, packs[0][0].shape[1] // 2
    keys = panel.shape[0]
    arrays = [p for pack in packs for p in pack]

    def body(*refs):
        refs = list(refs)
        pack_refs = [[refs.pop(0) for _ in pack] for pack in packs]
        panel_ref = refs.pop(0)
        dq_in = None if first else [refs.pop(0) for _ in range(n_packs)]
        sum_in = refs.pop(0) if add else None
        dq_out = [refs.pop(0) for _ in range(n_packs)]
        block_kernel(n_packs, first, add, pack_refs, panel_ref, dq_in, sum_in, dq_out, refs.pop(0))

    args = [*arrays, panel, *([] if first else dqs), *([total] if add else [])]
    aliases = {} if first else {len(arrays) + 1 + i: i for i in range(n_packs)}
    if add and out_type == F32:
        aliases[len(args) - 1] = n_packs
    vmem = pl.BlockSpec(memory_space=pltpu.VMEM)
    out = pl.pallas_call(
        body,
        out_shape=[jax.ShapeDtypeStruct((half, channels), F32)] * n_packs
        + [jax.ShapeDtypeStruct((keys, 2 * channels), out_type)],
        in_specs=[vmem] * len(args),
        out_specs=[vmem] * (n_packs + 1),
        input_output_aliases=aliases,
        cost_estimate=pl.CostEstimate(
            flops=10 * n_packs * half * keys * channels,
            bytes_accessed=2 * n_packs * half * channels * 2,
            transcendentals=n_packs * half * keys,
        ),
        compiler_params=pltpu.CompilerParams(vmem_limit_bytes=16 * 1024 * 1024),
    )(*args)
    return list(out[:n_packs]), out[n_packs]


def steps(queries, grad_out, attn_out, row_lse, keys, values):
    _, channels = queries.shape
    scale = channels ** (-0.5)
    core = lax.axis_index("kv")

    pack0, top, low, k0 = make_pack(core, queries, grad_out, attn_out, row_lse, keys, values)
    pack1 = trade(pack0, "slab_1", 0)
    pack2 = (trade(top, "slab_1", 1), trade(low, "slab_1", 1))
    pack3 = trade(pack1, "slab_1", 1)
    pack0, pack1, pack3 = (pack0,), (pack1,), (pack3,)

    zall = across(k0).reshape(-1, k0.shape[2])
    y1 = trade(zall, "slab_0", 0)
    near = jnp.concatenate([zall, y1])
    far = trade(near, "slab_0", 1)
    near_other = swap(near)
    far_other = swap(far)

    two = [pack0, pack1]
    b = [pack3]
    dqa, near_sum = block_work(two, near, None, None, F32)
    dqa, near_osum = block_work(two, near_other, dqa, None, F32)
    dqc, near_sum = block_work([pack2], near, None, near_sum, F32)
    dqc, near_osum = block_work([pack2], near_other, dqc, near_osum, F32)
    dqa, far_sum = block_work([*two, pack2], far, dqa + dqc, None, F32)
    dqa, far_osum = block_work([*two, pack2], far_other, dqa, None, F32)
    dqb, far_osum = block_work(b, far_other, None, far_osum, BF16)
    dqb, far_sum = block_work(b, far, dqb, far_sum, F32)
    dqb, near_osum = block_work(b, near_other, dqb, near_osum, BF16)
    dqb, near_sum = block_work(b, near, dqb, near_sum, F32)

    far_sum = far_sum + swap(far_osum).astype(F32)
    near_sum = near_sum + swap(near_osum).astype(F32)
    n1 = keys.shape[1]
    kept, sent = split_sum(near_sum, trade(far_sum.astype(BF16), "slab_0", 1))
    parts = across(rounded_sum(kept, trade(sent, "slab_0", 0), n1))
    grad_keys, grad_values = finish(parts, scale)

    got3 = trade(dqb[0].astype(BF16), "slab_1", 1).astype(F32)
    got2 = trade(dqa[2].astype(BF16), "slab_1", 1).astype(F32)
    got1 = trade((dqa[1] + got3).astype(BF16), "slab_1", 0).astype(F32)
    dq = ((dqa[0] + got2 + got1) * scale).astype(BF16)
    width = channels // 2
    keep = lax.dynamic_slice_in_dim(dq, core * width, width, 1)
    away = swap(lax.dynamic_slice_in_dim(dq, (1 - core) * width, width, 1))
    grad_queries = jnp.where(
        core == 0, jnp.concatenate([keep, away]), jnp.concatenate([away, keep])
    )
    return (grad_queries, grad_keys, grad_values)


def solution(mesh):
    torus = Mesh(
        mesh.devices.reshape(4, 4, 8, mesh.shape["kv"]), ("slab_0", "slab_1", "slab_2", "kv")
    )
    placed = (
        P(SLAB, None),
        P(SLAB, None),
        P(SLAB, None),
        P(SLAB),
        P("kv", SLAB, None),
        P("kv", SLAB, None),
    )
    return jax.shard_map(
        steps,
        mesh=torus,
        in_specs=placed,
        out_specs=(P(SLAB, "kv"), P("kv", SLAB, None), P("kv", SLAB, None)),
        check_vma=False,
    )
```

```python
import functools

import jax
import jax.numpy as jnp
from jax import lax
from jax.experimental import pallas as pl
from jax.experimental.pallas import tpu as pltpu
from jax.sharding import Mesh
from jax.sharding import PartitionSpec as P

SLAB = ("slab_0", "slab_1", "slab_2")
F32 = jnp.float32
BF16 = jnp.bfloat16


def neighbour(i, n, turn):
    if turn == 0:
        return i ^ 1
    return (i - 1) % n if i % 2 == 0 else (i + 1) % n


def trade(x, axis, turn):
    n = lax.axis_size(axis)
    pairs = []
    for i in range(n):
        for core in range(2):
            j = neighbour(i, n, (turn + core) % 2)
            pairs.append((2 * i + core, 2 * j + core))
    return lax.ppermute(x, (axis, "kv"), pairs)


def swap(x):
    return lax.ppermute(x, "kv", [(0, 1), (1, 0)])


def across(x):
    return lax.all_to_all(x, "slab_2", 0, 0, tiled=True)


def pack_kernel(
    core_ref, q_hbm, g_hbm, o_hbm, lse_hbm, k_hbm, v_hbm,
    out_ref, top_ref, low_ref, own_ref, o_half, lse_ref, kv_ref, sems,
):
    half, channels = o_half.shape
    core = core_ref[0]
    piece = 128
    n = half // piece
    copies = []
    for i in range(n):
        rows = pl.ds(pl.multiple_of(core * half + i * piece, piece), piece)
        to = slice(i * piece, (i + 1) * piece)
        copies.append(
            (
                pltpu.make_async_copy(g_hbm.at[rows, :], out_ref.at[to, channels:], sems.at[i]),
                pltpu.make_async_copy(o_hbm.at[rows, :], o_half.at[to, :], sems.at[n + i]),
                pltpu.make_async_copy(q_hbm.at[rows, :], out_ref.at[to, :channels], sems.at[2 * n + i]),
            )
        )
    small = [
        pltpu.make_async_copy(lse_hbm, lse_ref, sems.at[3 * n]),
        pltpu.make_async_copy(k_hbm.at[0], kv_ref.at[:, :channels], sems.at[3 * n + 1]),
        pltpu.make_async_copy(v_hbm.at[0], kv_ref.at[:, channels:], sems.at[3 * n + 2]),
    ]
    for copy in small:
        copy.start()
    for trio in copies:
        trio[0].start()
        trio[1].start()
    for trio in copies:
        trio[2].start()
    for copy in small:
        copy.wait()
    for i in range(own_ref.shape[0]):
        own_ref[i] = kv_ref[...]

    def line(first):
        return jnp.concatenate([lse_ref[i : i + 1, :] for i in range(first, first + n)], axis=1)

    lse = jnp.where(core == 0, line(0), line(n))
    pieces = []
    for i in range(n):
        copies[i][0].wait()
        copies[i][1].wait()
        to = slice(i * piece, (i + 1) * piece)
        product = out_ref[to, channels:].astype(F32) * o_half[to, :].astype(F32)
        column = jnp.sum(product, axis=1, keepdims=True)
        pieces.append(jnp.transpose(jnp.broadcast_to(column, (piece, 128)))[:1, :])
    stats = jnp.concatenate(pieces, axis=1)
    row = lax.broadcasted_iota(jnp.int32, (8, half), 0)
    for at, v in ((0, lse), (half, stats)):
        hi = v.astype(BF16).astype(F32)
        mid = (v - hi).astype(BF16).astype(F32)
        low = v - hi - mid
        terms = jnp.where(row == 0, hi, jnp.where(row == 1, mid, jnp.where(row == 2, low, 0.0)))
        out_ref[half:, at : at + half] = terms.astype(BF16)
    for trio in copies:
        trio[2].wait()
    cut = top_ref.shape[0]
    top_ref[...] = out_ref[:cut, :]
    low_ref[...] = out_ref[cut:, :]


def make_pack(core, queries, grad_out, attn_out, row_lse, keys, values):
    tokens, channels = queries.shape
    half = tokens // 2
    arrays = (queries, grad_out, attn_out, row_lse.reshape(-1, 128), keys, values)
    arrays = [pltpu.with_memory_space_constraint(a, pltpu.HBM) for a in arrays]
    hbm = pl.BlockSpec(memory_space=pltpu.HBM)
    vmem = pl.BlockSpec(memory_space=pltpu.VMEM)
    rows = keys.shape[1]
    return pl.pallas_call(
        pack_kernel,
        out_shape=[
            jax.ShapeDtypeStruct((half + 8, 2 * channels), BF16),
            jax.ShapeDtypeStruct((half * 192 // 512, 2 * channels), BF16),
            jax.ShapeDtypeStruct((half * 320 // 512 + 8, 2 * channels), BF16),
            jax.ShapeDtypeStruct((8, rows, 2 * channels), BF16),
        ],
        in_specs=[pl.BlockSpec(memory_space=pltpu.SMEM)] + [hbm] * 6,
        out_specs=[vmem] * 4,
        scratch_shapes=[
            pltpu.VMEM((half, channels), BF16),
            pltpu.VMEM((tokens // 128, 128), F32),
            pltpu.VMEM((rows, 2 * channels), BF16),
            pltpu.SemaphoreType.DMA((15,)),
        ],
        compiler_params=pltpu.CompilerParams(vmem_limit_bytes=16 * 1024 * 1024),
        name="pack",
    )(core.reshape(1), *arrays)


def split_sum_kernel(mine_ref, core_ref, got_ref, kept_ref, sent_ref):
    n = kept_ref.shape[0]
    kept_ref[...] = mine_ref[:n, :] + core_ref[:n, :].astype(F32) + got_ref[:n, :].astype(F32)
    low = mine_ref[n:, :] + core_ref[n:, :].astype(F32) + got_ref[n:, :].astype(F32)
    sent_ref[...] = low.astype(BF16)


def split_sum(mine, other_core, got):
    vmem = pl.BlockSpec(memory_space=pltpu.VMEM)
    half = (mine.shape[0] // 2, mine.shape[1])
    return pl.pallas_call(
        split_sum_kernel,
        out_shape=[jax.ShapeDtypeStruct(half, F32), jax.ShapeDtypeStruct(half, BF16)],
        in_specs=[vmem, vmem, vmem],
        out_specs=[vmem, vmem],
        compiler_params=pltpu.CompilerParams(vmem_limit_bytes=6 * 1024 * 1024),
        name="split_sum",
    )(mine, other_core, got)


def rounded_sum_kernel(mine_ref, got_ref, out_ref):
    total = mine_ref[...] + got_ref[...].astype(F32)
    out_ref[...] = total.astype(BF16).reshape(out_ref.shape)


def rounded_sum(mine, got, rows):
    vmem = pl.BlockSpec(memory_space=pltpu.VMEM)
    return pl.pallas_call(
        rounded_sum_kernel,
        out_shape=jax.ShapeDtypeStruct((got.shape[0] // rows, rows, got.shape[1]), BF16),
        in_specs=[vmem, vmem],
        compiler_params=pltpu.CompilerParams(vmem_limit_bytes=4 * 1024 * 1024),
        name="rounded_sum",
    )(mine, got)


def finish_kernel(scale, parts_ref, k_ref, v_ref):
    channels = k_ref.shape[2]
    own = jnp.sum(parts_ref[...].astype(F32), axis=0)
    k_ref[0] = (own[:, :channels] * scale).astype(BF16)
    v_ref[0] = own[:, channels:].astype(BF16)


def finish(parts, scale):
    rows, channels = parts.shape[1], parts.shape[2] // 2
    return pl.pallas_call(
        functools.partial(finish_kernel, scale),
        out_shape=[jax.ShapeDtypeStruct((1, rows, channels), BF16)] * 2,
        compiler_params=pltpu.CompilerParams(vmem_limit_bytes=4 * 1024 * 1024),
        name="finish",
    )(parts)


def dot(left, right, ld, rd):
    return lax.dot_general(left, right, (((ld,), (rd,)), ((), ())), preferred_element_type=F32)


def block_kernel(n_packs, first, add, pack_refs, panel_ref, dq_in, sum_in, dq_out, sum_out):
    half, channels = dq_out[0].shape
    log2e = 1.4426950408889634
    scale = channels ** (-0.5) * log2e
    k, v = panel_ref[:, :channels], panel_ref[:, channels:]
    dk, dv = None, None
    for i in range(n_packs):
        parts = pack_refs[i]
        last = parts[-1].shape[0] - 8
        q = [p[:, :channels] for p in parts[:-1]] + [parts[-1][:last, :channels]]
        g = [p[:, channels:] for p in parts[:-1]] + [parts[-1][:last, channels:]]
        q = q[0] if len(q) == 1 else jnp.concatenate(q)
        g = g[0] if len(g) == 1 else jnp.concatenate(g)
        both = jnp.sum(parts[-1][last:, :].astype(F32), axis=0, keepdims=True)
        lse, stats = both[:, :half] * log2e, both[:, half:]
        probs = jnp.exp2(dot(k, q, 1, 1) * scale - lse)
        dscores = (probs * (dot(v, g, 1, 1) - stats)).astype(BF16)
        dk_i = dot(dscores, q, 1, 0)
        dv_i = dot(probs.astype(BF16), g, 1, 0)
        dk = dk_i if dk is None else dk + dk_i
        dv = dv_i if dv is None else dv + dv_i
        dq = dot(dscores, k, 0, 0)
        dq_out[i][...] = dq if first else dq_in[i][...] + dq
    if add:
        dk, dv = dk + sum_in[:, :channels], dv + sum_in[:, channels:]
    sum_out[:, :channels] = dk.astype(sum_out.dtype)
    sum_out[:, channels:] = dv.astype(sum_out.dtype)


def block_work(packs, panel, dqs, total, out_type, after=()):
    n_packs, first, add = len(packs), dqs is None, total is not None
    half, channels = sum(p.shape[0] for p in packs[0]) - 8, packs[0][0].shape[1] // 2
    keys = panel.shape[0]
    arrays = [p for pack in packs for p in pack]

    def body(*refs):
        refs = list(refs)
        pack_refs = [[refs.pop(0) for _ in pack] for pack in packs]
        panel_ref = refs.pop(0)
        dq_in = None if first else [refs.pop(0) for _ in range(n_packs)]
        sum_in = refs.pop(0) if add else None
        refs = refs[len(after) :]
        dq_out = [refs.pop(0) for _ in range(n_packs)]
        block_kernel(n_packs, first, add, pack_refs, panel_ref, dq_in, sum_in, dq_out, refs.pop(0))

    args = [*arrays, panel, *([] if first else dqs), *([total] if add else []), *after]
    aliases = {} if first else {len(arrays) + 1 + i: i for i in range(n_packs)}
    if add and out_type == F32:
        aliases[len(args) - 1 - len(after)] = n_packs
    vmem = pl.BlockSpec(memory_space=pltpu.VMEM)
    out = pl.pallas_call(
        body,
        out_shape=[jax.ShapeDtypeStruct((half, channels), F32)] * n_packs
        + [jax.ShapeDtypeStruct((keys, 2 * channels), out_type)],
        in_specs=[vmem] * len(args),
        out_specs=[vmem] * (n_packs + 1),
        input_output_aliases=aliases,
        cost_estimate=pl.CostEstimate(
            flops=10 * n_packs * half * keys * channels,
            bytes_accessed=2 * n_packs * half * channels * 2,
            transcendentals=n_packs * half * keys,
        ),
        compiler_params=pltpu.CompilerParams(vmem_limit_bytes=16 * 1024 * 1024),
    )(*args)
    return list(out[:n_packs]), out[n_packs]


def steps(queries, grad_out, attn_out, row_lse, keys, values):
    tokens, channels = queries.shape
    scale = channels ** (-0.5)
    core = lax.axis_index("kv")

    pack0, top, low, k0 = make_pack(core, queries, grad_out, attn_out, row_lse, keys, values)
    pack1 = trade(pack0, "slab_1", 0)
    pack2 = (trade(top, "slab_1", 1), trade(low, "slab_1", 1))
    pack3 = trade(pack1, "slab_1", 1)
    pack0, pack1, pack3 = (pack0,), (pack1,), (pack3,)

    zall = across(k0).reshape(-1, k0.shape[2])
    y1 = trade(zall, "slab_0", 0)
    near = jnp.concatenate([zall, y1])
    far = trade(near, "slab_0", 1)
    near_other = swap(near)
    far_other = swap(far)

    half = tokens // 2
    two = [pack0, pack1]
    b = [pack3]
    seen = pack1[0][half:, :128] * 2
    dqa, near_sum = block_work(two, near, None, None, F32, (seen,))
    dqa, near_osum = block_work(two, near_other, dqa, None, F32)
    dqc, near_sum = block_work([pack2], near, None, near_sum, F32, (near_osum,))
    dqc, near_osum = block_work([pack2], near_other, dqc, near_osum, F32)
    dqa, far_sum = block_work([*two, pack2], far, dqa + dqc, None, F32)
    dqa, far_osum = block_work([*two, pack2], far_other, dqa, None, F32)
    dqb, far_osum = block_work(b, far_other, None, far_osum, BF16)
    dqb, far_sum = block_work(b, far, dqb, far_sum, F32)
    dqb, near_osum = block_work(b, near_other, dqb, near_osum, BF16)
    dqb, near_sum = block_work(b, near, dqb, near_sum, F32)

    far_sum = far_sum + swap(far_osum).astype(F32)
    near_got = swap(near_osum)
    n1 = keys.shape[1]
    kept, sent = split_sum(near_sum, near_got, trade(far_sum.astype(BF16), "slab_0", 1))
    parts = across(rounded_sum(kept, trade(sent, "slab_0", 0), n1))
    grad_keys, grad_values = finish(parts, scale)

    got3 = trade(dqb[0].astype(BF16), "slab_1", 1).astype(F32)
    got2 = trade(dqa[2].astype(BF16), "slab_1", 1).astype(F32)
    got1 = trade((dqa[1] + got3).astype(BF16), "slab_1", 0).astype(F32)
    dq = ((dqa[0] + got2 + got1) * scale).astype(BF16)
    width = channels // 2
    keep = lax.dynamic_slice_in_dim(dq, core * width, width, 1)
    away = swap(lax.dynamic_slice_in_dim(dq, (1 - core) * width, width, 1))
    grad_queries = jnp.where(
        core == 0, jnp.concatenate([keep, away]), jnp.concatenate([away, keep])
    )
    return (grad_queries, grad_keys, grad_values)


def solution(mesh):
    torus = Mesh(
        mesh.devices.reshape(4, 4, 8, mesh.shape["kv"]), ("slab_0", "slab_1", "slab_2", "kv")
    )
    placed = (
        P(SLAB, None),
        P(SLAB, None),
        P(SLAB, None),
        P(SLAB),
        P("kv", SLAB, None),
        P("kv", SLAB, None),
    )
    return jax.shard_map(
        steps,
        mesh=torus,
        in_specs=placed,
        out_specs=(P(SLAB, "kv"), P("kv", SLAB, None), P("kv", SLAB, None)),
        check_vma=False,
    )
```

```python
import functools

import jax
import jax.numpy as jnp
from jax import lax
from jax.experimental import pallas as pl
from jax.experimental.pallas import tpu as pltpu
from jax.sharding import Mesh
from jax.sharding import PartitionSpec as P

SLAB = ("slab_0", "slab_1", "slab_2")
F32 = jnp.float32
BF16 = jnp.bfloat16


def neighbour(i, n, turn):
    if turn == 0:
        return i ^ 1
    return (i - 1) % n if i % 2 == 0 else (i + 1) % n


def trade(x, axis, turn):
    n = lax.axis_size(axis)
    pairs = []
    for i in range(n):
        for core in range(2):
            j = neighbour(i, n, (turn + core) % 2)
            pairs.append((2 * i + core, 2 * j + core))
    return lax.ppermute(x, (axis, "kv"), pairs)


def swap(x):
    return lax.ppermute(x, "kv", [(0, 1), (1, 0)])


def across(x):
    return lax.all_to_all(x, "slab_2", 0, 0, tiled=True)


def pack_kernel(
    core_ref, q_hbm, g_hbm, o_hbm, lse_hbm, k_hbm, v_hbm,
    out_ref, top_ref, low_ref, own_ref, o_half, lse_ref, kv_ref, sems,
):
    half, channels = o_half.shape
    core = core_ref[0]
    piece = 128
    n = half // piece
    copies = []
    for i in range(n):
        rows = pl.ds(pl.multiple_of(core * half + i * piece, piece), piece)
        to = slice(i * piece, (i + 1) * piece)
        copies.append(
            (
                pltpu.make_async_copy(g_hbm.at[rows, :], out_ref.at[to, channels:], sems.at[i]),
                pltpu.make_async_copy(o_hbm.at[rows, :], o_half.at[to, :], sems.at[n + i]),
                pltpu.make_async_copy(q_hbm.at[rows, :], out_ref.at[to, :channels], sems.at[2 * n + i]),
            )
        )
    small = [
        pltpu.make_async_copy(lse_hbm, lse_ref, sems.at[3 * n]),
        pltpu.make_async_copy(k_hbm.at[0], kv_ref.at[:, :channels], sems.at[3 * n + 1]),
        pltpu.make_async_copy(v_hbm.at[0], kv_ref.at[:, channels:], sems.at[3 * n + 2]),
    ]
    for copy in small:
        copy.start()
    for trio in copies:
        trio[0].start()
        trio[1].start()
    for trio in copies:
        trio[2].start()
    for copy in small:
        copy.wait()
    for i in range(own_ref.shape[0]):
        own_ref[i] = kv_ref[...]

    def line(first):
        return jnp.concatenate([lse_ref[i : i + 1, :] for i in range(first, first + n)], axis=1)

    lse = jnp.where(core == 0, line(0), line(n))
    pieces = []
    for i in range(n):
        copies[i][0].wait()
        copies[i][1].wait()
        to = slice(i * piece, (i + 1) * piece)
        product = out_ref[to, channels:].astype(F32) * o_half[to, :].astype(F32)
        column = jnp.sum(product, axis=1, keepdims=True)
        pieces.append(jnp.transpose(jnp.broadcast_to(column, (piece, 128)))[:1, :])
    stats = jnp.concatenate(pieces, axis=1)
    row = lax.broadcasted_iota(jnp.int32, (8, half), 0)
    for at, v in ((0, lse), (half, stats)):
        hi = v.astype(BF16).astype(F32)
        mid = (v - hi).astype(BF16).astype(F32)
        low = v - hi - mid
        terms = jnp.where(row == 0, hi, jnp.where(row == 1, mid, jnp.where(row == 2, low, 0.0)))
        out_ref[half:, at : at + half] = terms.astype(BF16)
    for trio in copies:
        trio[2].wait()
    cut = top_ref.shape[0]
    top_ref[...] = out_ref[:cut, :]
    low_ref[...] = out_ref[cut:, :]


def make_pack(core, queries, grad_out, attn_out, row_lse, keys, values):
    tokens, channels = queries.shape
    half = tokens // 2
    arrays = (queries, grad_out, attn_out, row_lse.reshape(-1, 128), keys, values)
    arrays = [pltpu.with_memory_space_constraint(a, pltpu.HBM) for a in arrays]
    hbm = pl.BlockSpec(memory_space=pltpu.HBM)
    vmem = pl.BlockSpec(memory_space=pltpu.VMEM)
    rows = keys.shape[1]
    return pl.pallas_call(
        pack_kernel,
        out_shape=[
            jax.ShapeDtypeStruct((half + 8, 2 * channels), BF16),
            jax.ShapeDtypeStruct((half * 192 // 512, 2 * channels), BF16),
            jax.ShapeDtypeStruct((half * 320 // 512 + 8, 2 * channels), BF16),
            jax.ShapeDtypeStruct((8, rows, 2 * channels), BF16),
        ],
        in_specs=[pl.BlockSpec(memory_space=pltpu.SMEM)] + [hbm] * 6,
        out_specs=[vmem] * 4,
        scratch_shapes=[
            pltpu.VMEM((half, channels), BF16),
            pltpu.VMEM((tokens // 128, 128), F32),
            pltpu.VMEM((rows, 2 * channels), BF16),
            pltpu.SemaphoreType.DMA((15,)),
        ],
        compiler_params=pltpu.CompilerParams(vmem_limit_bytes=10 * 1024 * 1024),
        name="pack",
    )(core.reshape(1), *arrays)


def split_sum_kernel(mine_ref, got_ref, kept_ref, sent_ref):
    n = kept_ref.shape[0]
    kept_ref[...] = mine_ref[:n, :] + got_ref[:n, :].astype(F32)
    sent_ref[...] = (mine_ref[n:, :] + got_ref[n:, :].astype(F32)).astype(BF16)


def split_sum(mine, got):
    vmem = pl.BlockSpec(memory_space=pltpu.VMEM)
    half = (mine.shape[0] // 2, mine.shape[1])
    return pl.pallas_call(
        split_sum_kernel,
        out_shape=[jax.ShapeDtypeStruct(half, F32), jax.ShapeDtypeStruct(half, BF16)],
        in_specs=[vmem, vmem],
        out_specs=[vmem, vmem],
        compiler_params=pltpu.CompilerParams(vmem_limit_bytes=4 * 1024 * 1024),
        name="split_sum",
    )(mine, got)


def rounded_sum_kernel(mine_ref, got_ref, out_ref):
    total = mine_ref[...] + got_ref[...].astype(F32)
    out_ref[...] = total.astype(BF16).reshape(out_ref.shape)


def rounded_sum(mine, got, rows):
    vmem = pl.BlockSpec(memory_space=pltpu.VMEM)
    return pl.pallas_call(
        rounded_sum_kernel,
        out_shape=jax.ShapeDtypeStruct((got.shape[0] // rows, rows, got.shape[1]), BF16),
        in_specs=[vmem, vmem],
        compiler_params=pltpu.CompilerParams(vmem_limit_bytes=4 * 1024 * 1024),
        name="rounded_sum",
    )(mine, got)


def finish_kernel(scale, parts_ref, k_ref, v_ref):
    channels = k_ref.shape[2]
    own = jnp.sum(parts_ref[...].astype(F32), axis=0)
    k_ref[0] = (own[:, :channels] * scale).astype(BF16)
    v_ref[0] = own[:, channels:].astype(BF16)


def finish(parts, scale):
    rows, channels = parts.shape[1], parts.shape[2] // 2
    return pl.pallas_call(
        functools.partial(finish_kernel, scale),
        out_shape=[jax.ShapeDtypeStruct((1, rows, channels), BF16)] * 2,
        compiler_params=pltpu.CompilerParams(vmem_limit_bytes=4 * 1024 * 1024),
        name="finish",
    )(parts)


def dot(left, right, ld, rd):
    return lax.dot_general(left, right, (((ld,), (rd,)), ((), ())), preferred_element_type=F32)


def block_kernel(n_packs, first, add, pack_refs, panel_ref, dq_in, sum_in, dq_out, sum_out):
    half, channels = dq_out[0].shape
    log2e = 1.4426950408889634
    scale = channels ** (-0.5) * log2e
    k, v = panel_ref[:, :channels], panel_ref[:, channels:]
    dk, dv = None, None
    for i in range(n_packs):
        parts = pack_refs[i]
        last = parts[-1].shape[0] - 8
        q = [p[:, :channels] for p in parts[:-1]] + [parts[-1][:last, :channels]]
        g = [p[:, channels:] for p in parts[:-1]] + [parts[-1][:last, channels:]]
        q = q[0] if len(q) == 1 else jnp.concatenate(q)
        g = g[0] if len(g) == 1 else jnp.concatenate(g)
        both = jnp.sum(parts[-1][last:, :].astype(F32), axis=0, keepdims=True)
        lse, stats = both[:, :half] * log2e, both[:, half:]
        probs = jnp.exp2(dot(k, q, 1, 1) * scale - lse)
        dscores = (probs * (dot(v, g, 1, 1) - stats)).astype(BF16)
        dk_i = dot(dscores, q, 1, 0)
        dv_i = dot(probs.astype(BF16), g, 1, 0)
        dk = dk_i if dk is None else dk + dk_i
        dv = dv_i if dv is None else dv + dv_i
        dq = dot(dscores, k, 0, 0)
        dq_out[i][...] = dq if first else dq_in[i][...] + dq
    if add:
        dk, dv = dk + sum_in[:, :channels], dv + sum_in[:, channels:]
    sum_out[:, :channels] = dk.astype(sum_out.dtype)
    sum_out[:, channels:] = dv.astype(sum_out.dtype)


def block_work(packs, panel, dqs, total, out_type, after=()):
    n_packs, first, add = len(packs), dqs is None, total is not None
    half, channels = sum(p.shape[0] for p in packs[0]) - 8, packs[0][0].shape[1] // 2
    keys = panel.shape[0]
    arrays = [p for pack in packs for p in pack]

    def body(*refs):
        refs = list(refs)
        pack_refs = [[refs.pop(0) for _ in pack] for pack in packs]
        panel_ref = refs.pop(0)
        dq_in = None if first else [refs.pop(0) for _ in range(n_packs)]
        sum_in = refs.pop(0) if add else None
        refs = refs[len(after) :]
        dq_out = [refs.pop(0) for _ in range(n_packs)]
        block_kernel(n_packs, first, add, pack_refs, panel_ref, dq_in, sum_in, dq_out, refs.pop(0))

    args = [*arrays, panel, *([] if first else dqs), *([total] if add else []), *after]
    aliases = {} if first else {len(arrays) + 1 + i: i for i in range(n_packs)}
    if add and out_type == F32:
        aliases[len(args) - 1 - len(after)] = n_packs
    vmem = pl.BlockSpec(memory_space=pltpu.VMEM)
    out = pl.pallas_call(
        body,
        out_shape=[jax.ShapeDtypeStruct((half, channels), F32)] * n_packs
        + [jax.ShapeDtypeStruct((keys, 2 * channels), out_type)],
        in_specs=[vmem] * len(args),
        out_specs=[vmem] * (n_packs + 1),
        input_output_aliases=aliases,
        cost_estimate=pl.CostEstimate(
            flops=10 * n_packs * half * keys * channels,
            bytes_accessed=2 * n_packs * half * channels * 2,
            transcendentals=n_packs * half * keys,
        ),
        compiler_params=pltpu.CompilerParams(vmem_limit_bytes=10 * 1024 * 1024),
    )(*args)
    return list(out[:n_packs]), out[n_packs]


def steps(queries, grad_out, attn_out, row_lse, keys, values):
    tokens, channels = queries.shape
    scale = channels ** (-0.5)
    core = lax.axis_index("kv")

    pack0, top, low, k0 = make_pack(core, queries, grad_out, attn_out, row_lse, keys, values)
    pack1 = trade(pack0, "slab_1", 0)
    pack2 = (trade(top, "slab_1", 1), trade(low, "slab_1", 1))
    pack3 = trade(pack1, "slab_1", 1)
    pack0, pack1, pack3 = (pack0,), (pack1,), (pack3,)

    zall = across(k0).reshape(-1, k0.shape[2])
    y1 = trade(zall, "slab_0", 0)
    near = jnp.concatenate([zall, y1])
    far = trade(near, "slab_0", 1)
    near_other = swap(near)
    far_other = swap(far)

    half = tokens // 2
    two = [pack0, pack1]
    b = [pack3]
    seen = pack1[0][half:, :128] * 2
    dqa, near_sum = block_work(two, near, None, None, F32, (seen,))
    dqa, near_osum = block_work(two, near_other, dqa, None, F32)
    dqc, near_sum = block_work([pack2], near, None, near_sum, F32, (near_osum,))
    dqc, near_osum = block_work([pack2], near_other, dqc, near_osum, F32)
    dqa, far_sum = block_work([*two, pack2], far, dqa + dqc, None, F32)
    dqa, far_osum = block_work([*two, pack2], far_other, dqa, None, F32)
    dqb, far_osum = block_work(b, far_other, None, far_osum, BF16)
    dqb, far_sum = block_work(b, far, dqb, far_sum, F32)
    dqb, near_osum = block_work(b, near_other, dqb, near_osum, BF16)
    dqb, near_sum = block_work(b, near, dqb, near_sum, F32)

    far_sum = far_sum + swap(far_osum).astype(F32)
    near_sum = near_sum + swap(near_osum).astype(F32)
    n1 = keys.shape[1]
    kept, sent = split_sum(near_sum, trade(far_sum.astype(BF16), "slab_0", 1))
    parts = across(rounded_sum(kept, trade(sent, "slab_0", 0), n1))
    grad_keys, grad_values = finish(parts, scale)

    got3 = trade(dqb[0].astype(BF16), "slab_1", 1).astype(F32)
    got2 = trade(dqa[2].astype(BF16), "slab_1", 1).astype(F32)
    got1 = trade((dqa[1] + got3).astype(BF16), "slab_1", 0).astype(F32)
    dq = ((dqa[0] + got2 + got1) * scale).astype(BF16)
    width = channels // 2
    keep = lax.dynamic_slice_in_dim(dq, core * width, width, 1)
    away = swap(lax.dynamic_slice_in_dim(dq, (1 - core) * width, width, 1))
    grad_queries = jnp.where(
        core == 0, jnp.concatenate([keep, away]), jnp.concatenate([away, keep])
    )
    return (grad_queries, grad_keys, grad_values)


def solution(mesh):
    torus = Mesh(
        mesh.devices.reshape(4, 4, 8, mesh.shape["kv"]), ("slab_0", "slab_1", "slab_2", "kv")
    )
    placed = (
        P(SLAB, None),
        P(SLAB, None),
        P(SLAB, None),
        P(SLAB),
        P("kv", SLAB, None),
        P("kv", SLAB, None),
    )
    return jax.shard_map(
        steps,
        mesh=torus,
        in_specs=placed,
        out_specs=(P(SLAB, "kv"), P("kv", SLAB, None), P("kv", SLAB, None)),
        check_vma=False,
    )
```
